512 devices in a mesh: box: 32 (over y, z_hi, core), grp: 16 (over z_lo, x).
Axes of the slice: x: 4, y: 8, z: 8 (z_hi: 2, z_lo: 4; z = z_hi * 4 + z_lo), core: 2. Of those that a mesh axis runs over, the one named last changes fastest.
Arguments:
- impedance: bfloat16 [2, 32, 1, 2048, 2048], P(None, 'box', None, None, 'grp'), may hold values from -3 to 3
- face_order: int32 [32, 1, 16], replicated, may hold values from 0 to 15, each once within a row
Outputs:
- merged: bfloat16 [2, 32, 1, 4096, 2048], P(None, 'box', None, None, 'grp')
The draws below stay inside these ranges and needn't reach their ends.
Inputs may be any that keep to these rules, and one draw needn't show every extreme that they name: `face_order`: each row lists the 16 face blocks of one box once; its first 3 entries are the blocks on the face shared with the sibling, the k-th facing the sibling's k-th.
All inputs are finite; a program needn't handle non-finite values.
Results may differ from the reference program's by a relative error of at most 0.0035.
Values may be sent and summed in bfloat16 or wider, within the bound.
No kernel may reach another device: no remote copies, remote signals or barrier semaphores. Data moves between devices by JAX's collectives and lax.ppermute only.
A program may use at most 64 MiB of HBM per device.

```python
import jax
import jax.numpy as jnp
from jax import lax

NB = 2048
BLK = 128
FB = 16
MB = 3
NS_STEPS = 2
BOX_DEV = 1
GROUPS = 32


def draw_impedance(key, part):
    full_shape = (2, GROUPS, BOX_DEV, NB, NB)
    entries = jax.random.truncated_normal(key, -3.0, 3.0, full_shape, jnp.float32)
    return entries.astype(jnp.bfloat16)


def setup_inputs(seed: int = 0) -> dict:
    arg_keys = jax.random.split(jax.random.key(seed), 3)
    impedance = draw_impedance(jax.random.fold_in(arg_keys[2], 71), 0)
    face_order = jax.vmap(lambda own: jax.random.permutation(own, FB))(jax.random.split(arg_keys[1], GROUPS * BOX_DEV)).reshape((GROUPS, BOX_DEV, FB)).astype(jnp.int32)
    return {"impedance": impedance, "face_order": face_order}


HIGHEST_PREC = lax.Precision.HIGHEST


def complex_dot(left_mat, right_mat, precision):
    real_part = jnp.dot(left_mat[0], right_mat[0], precision=precision, preferred_element_type=jnp.float32) - jnp.dot(left_mat[1], right_mat[1], precision=precision, preferred_element_type=jnp.float32)
    imag_part = jnp.dot(left_mat[0], right_mat[1], precision=precision, preferred_element_type=jnp.float32) + jnp.dot(left_mat[1], right_mat[0], precision=precision, preferred_element_type=jnp.float32)
    return jnp.stack([real_part, imag_part])


def iface_index(face_list):
    return (face_list[:MB, None] * BLK + jnp.arange(BLK, dtype=jnp.int32)[None, :]).reshape(MB * BLK).astype(jnp.int32)


def exterior_mask(face_list):
    block_ids = jnp.arange(NB, dtype=jnp.int32) // BLK
    on_face = jnp.any(block_ids[:, None] == face_list[None, :MB], axis=1)
    return jnp.where(on_face, jnp.float32(0.0), jnp.float32(1.0)).astype(jnp.float32)


def merge_pair(pair_item):
    box_maps, orders = pair_item
    coupling_sq = 1.0 / NB
    coupling = NB ** -0.5
    iface_len = MB * BLK
    identity = jnp.eye(iface_len, dtype=jnp.float32)
    ident_pair = jnp.stack([identity, jnp.zeros_like(identity)])
    point_lists = [iface_index(orders[0]), iface_index(orders[1])]
    ext_masks = [exterior_mask(orders[0]), exterior_mask(orders[1])]
    iface_cols = [box_maps[0][:, :, point_lists[0]], box_maps[1][:, :, point_lists[1]]]
    blocks = [iface_cols[0][:, point_lists[0], :], iface_cols[1][:, point_lists[1], :]]
    iface_rows = [box_maps[0][:, point_lists[0], :], box_maps[1][:, point_lists[1], :]]
    results = []
    for side_idx in range(2):
        twin_idx = 1 - side_idx
        coupled = complex_dot(blocks[side_idx].astype(jnp.float32), blocks[twin_idx].astype(jnp.float32), HIGHEST_PREC)
        system = ident_pair - coupling_sq * coupled
        inverse = ident_pair
        for iteration in range(NS_STEPS):
            inverse = 2.0 * inverse - complex_dot(complex_dot(inverse, system, HIGHEST_PREC), inverse, HIGHEST_PREC)
        incoming = iface_rows[side_idx].astype(jnp.float32) * ext_masks[side_idx][None, None, :]
        response = complex_dot(inverse, incoming, HIGHEST_PREC)
        echoed = complex_dot(blocks[twin_idx].astype(jnp.float32), response, HIGHEST_PREC)
        own_out = box_maps[side_idx].astype(jnp.float32) * ext_masks[side_idx][None, None, :] + coupling_sq * complex_dot(iface_cols[side_idx], echoed.astype(jnp.bfloat16), None)
        cross_out = -coupling * complex_dot(iface_cols[twin_idx], response.astype(jnp.bfloat16), None)
        if side_idx == 0:
            column = jnp.concatenate([own_out, cross_out], axis=1)
        else:
            column = jnp.concatenate([cross_out, own_out], axis=1)
        results.append(column.astype(jnp.bfloat16))
    return jnp.stack(results)


def reference(impedance, face_order):
    pair_count = GROUPS // 2
    box_maps = impedance.reshape(2, pair_count, 2, BOX_DEV, NB, NB).transpose(1, 3, 2, 0, 4, 5).reshape(pair_count * BOX_DEV, 2, 2, NB, NB)
    orders = face_order.reshape(pair_count, 2, BOX_DEV, FB).transpose(0, 2, 1, 3).reshape(pair_count * BOX_DEV, 2, FB)
    merged = lax.map(merge_pair, (box_maps, orders))
    merged = merged.reshape(pair_count, BOX_DEV, 2, 2, 2 * NB, NB).transpose(3, 0, 2, 1, 4, 5)
    return merged.reshape(2, GROUPS, BOX_DEV, 2 * NB, NB)
```

```python
import functools

import jax
import jax.numpy as jnp
from jax import lax
from jax.experimental import pallas as pl
from jax.experimental.pallas import tpu as pltpu
from jax.sharding import PartitionSpec as P

BLK = 128
MB = 3
SUB = 8


SLOTS = (((0, 1), (0, 1)), ((0, 3), (2, 3)), ((3, 2), (0, 1)), ((1, 2), (2, 3)))


def exchange(block, axis, mask):
    count = lax.axis_size(axis)
    return lax.ppermute(block, axis, [(i, i ^ mask) for i in range(count)])


def turned(pair, width):
    return jnp.concatenate([-pair[:, width:], pair[:, :width]], axis=1)


def dot(a, b):
    return jnp.dot(a, b, preferred_element_type=jnp.float32)


def two_terms(v):
    high = v.astype(jnp.bfloat16)
    low = (v - high.astype(jnp.float32)).astype(jnp.bfloat16)
    return high, low


def solve_kernel(sc, own, q1, q2, s1, s2, t1, t2, u1, u2, resp, echo, zb, zs, *, scale):
    width = own.shape[-1]
    x, z = sc[6], sc[7]
    for dst, arrays, base in ((zb, (q1, q2, s1, s2), 0), (zs, (t1, t2, u1, u2), MB)):
        for arr, (xm, zm) in zip(arrays, SLOTS):
            for a in range(2):
                for b in range(2):
                    at = (jnp.bitwise_xor(x, xm[a]) * 4 + jnp.bitwise_xor(z, zm[b])) * SUB
                    for j in range(MB):
                        face = sc[base + j]
                        rows = pl.ds(pl.multiple_of(j * BLK + at, SUB), SUB)
                        for p in range(2):
                            dst[p, rows, :] = arr[a, b, p, face].astype(jnp.float32)
    ext = sc[9].astype(jnp.float32)
    parts = []
    for p in range(2):
        parts.append(
            jnp.concatenate(
                [own[p, sc[j]].astype(jnp.float32).reshape(BLK, width) for j in range(MB)], axis=0
            )
        )
    start = jnp.concatenate(parts, axis=1) * ext
    zbr, zbi = zb[0].astype(jnp.bfloat16), zb[1].astype(jnp.bfloat16)
    zsr, zsi = zs[0].astype(jnp.bfloat16), zs[1].astype(jnp.bfloat16)

    def times(zr, zi, v, exact=False):
        if exact:
            h = v.astype(jnp.bfloat16)
            return dot(zr, h) + dot(zi, turned(h, width))
        h, l = two_terms(v)
        return (dot(zr, l) + dot(zi, turned(l, width))) + (dot(zr, h) + dot(zi, turned(h, width)))

    v = start
    for step in range(3):
        v = start + scale * times(zbr, zbi, times(zsr, zsi, v, exact=step == 0))
    resp[...] = v.astype(jnp.bfloat16)
    echo[...] = times(zsr, zsi, v).astype(jnp.bfloat16)


def merge_kernel(sc, own, resp, echo, q1, q2, s1, s2, t1, t2, u1, u2, out, *, points):
    width = own.shape[-1]
    x, z, parity = sc[6], sc[7], sc[8]
    ext = sc[9].astype(jnp.float32)
    e1, r1 = echo[...], resp[...]
    e2, r2 = turned(e1, width), turned(r1, width)
    for kind, arrays, left, right in (
        (0, (q1, q2, s1, s2), e1, e2),
        (1, (t1, t2, u1, u2), r1, r2),
    ):
        half = jnp.bitwise_xor(parity, kind)
        for arr, (xm, zm) in zip(arrays, SLOTS):
            for a in range(2):
                rows = 2 * BLK
                zr = arr[a, :, 0].reshape(rows, MB * BLK)
                zi = arr[a, :, 1].reshape(rows, MB * BLK)
                acc = dot(zr, left) + dot(zi, right)
                for b in range(2):
                    at = jnp.bitwise_xor(x, xm[a]) * 4 + jnp.bitwise_xor(z, zm[b])
                    for p in range(2):
                        val = acc[b * BLK : (b + 1) * BLK, p * width : (p + 1) * width]
                        val = val.reshape(BLK // SUB, SUB, width)
                        if kind == 0:
                            val = own[p, :, at].astype(jnp.float32) * ext + val * (1.0 / points)
                        else:
                            val = val * -(points ** -0.5)
                        out[p, half, :, at] = val.astype(jnp.bfloat16)


def shards(impedance, face_order):
    own_cols = impedance[:, 0, 0]
    points, width = own_cols.shape[1:]
    faces = points // BLK
    box_here = lax.axis_index("box")
    grp_here = lax.axis_index("grp")
    parity = box_here % 2
    own_order = lax.dynamic_index_in_dim(face_order, box_here, 0, keepdims=False)[0]
    twin_order = lax.dynamic_index_in_dim(
        face_order, jnp.bitwise_xor(box_here, 1), 0, keepdims=False
    )[0]
    first = grp_here * width // BLK
    ext = jnp.where(jnp.any(own_order[:MB] == first), 0, 1).astype(jnp.int32)
    scalars = jnp.concatenate(
        [
            own_order[:MB],
            twin_order[:MB],
            jnp.stack([grp_here % 4, grp_here // 4, parity, ext]).astype(jnp.int32),
        ]
    )
    tiles = own_cols.reshape(2, faces, 4, 4, SUB, width)
    pieces = tiles.transpose(3, 2, 0, 1, 4, 5).reshape(16, 2, faces, SUB, width)
    spread = lax.all_to_all(pieces, "grp", 0, 0, tiled=True)
    mine = jnp.concatenate(
        [lax.dynamic_index_in_dim(spread, own_order[j], 0, keepdims=False) for j in range(MB)],
        axis=-1,
    )
    z1, z2, z3 = (exchange(mine, "grp", 4 * m) for m in (1, 2, 3))
    h1, h2 = jnp.stack([mine, z1]), jnp.stack([z2, z3])
    q1 = jnp.stack([h1, exchange(h1, "grp", 1)])
    q2 = jnp.stack([h2, exchange(h2, "grp", 3)])
    s1 = exchange(q1, "grp", 3)
    s2 = exchange(q2, "grp", 1)
    gathered = [q1, q2, s1, s2]
    gathered += [exchange(g, "box", 1) for g in gathered]
    own_tiles = own_cols.reshape(2, faces, BLK // SUB, SUB, width)
    smem = pl.BlockSpec(memory_space=pltpu.SMEM)
    vmem = pl.BlockSpec(memory_space=pltpu.VMEM)
    iface = MB * BLK
    small = jax.ShapeDtypeStruct((iface, 2 * width), jnp.bfloat16)
    resp, echo = pl.pallas_call(
        functools.partial(solve_kernel, scale=1.0 / points),
        out_shape=(small, small),
        in_specs=[smem] + [vmem] * 9,
        out_specs=(vmem, vmem),
        scratch_shapes=[pltpu.VMEM((2, iface, iface), jnp.float32)] * 2,
        name="solve",
    )(scalars, own_tiles, *gathered)
    flat = [g.reshape(2, 2, 2, BLK, iface) for g in gathered]
    out = pl.pallas_call(
        functools.partial(merge_kernel, points=points),
        out_shape=jax.ShapeDtypeStruct((2, 2, faces, BLK // SUB, SUB, width), jnp.bfloat16),
        in_specs=[smem] + [vmem] * 11,
        out_specs=vmem,
        name="merge",
    )(scalars, own_tiles, resp, echo, *flat)
    return out.reshape(2, 1, 1, 2 * points, width)


def solution(mesh):
    in_specs = (P(None, "box", None, None, "grp"), P())
    out_specs = P(None, "box", None, None, "grp")
    return jax.shard_map(shards, mesh=mesh, in_specs=in_specs, out_specs=out_specs, check_vma=False)
```

```python
import functools

import jax
import jax.numpy as jnp
from jax import lax
from jax.experimental import pallas as pl
from jax.experimental.pallas import tpu as pltpu
from jax.sharding import PartitionSpec as P


BLK = 128
MB = 3
IFACE = MB * BLK

PLACES = (
    (0, pl.ds(0, 2), pl.ds(0, 2), 0),
    (0, pl.ds(2, 3), 0, pl.ds(1, 3)),
    (0, pl.ds(5, 2), pl.ds(2, 2), 0),
    (1, pl.ds(0, 3), 1, pl.ds(1, 3)),
    (2, pl.ds(0, 2), pl.ds(2, 2), 1),
    (3, pl.ds(0, 2), pl.ds(2, 2), 3),
    (4, pl.ds(0, 2), pl.ds(2, 2), 2),
)


def exchange(block, axis, mask):
    count = lax.axis_size(axis)
    return lax.ppermute(block, axis, [(i, i ^ mask) for i in range(count)])


def stacked(pair, width):
    turned = jnp.concatenate([-pair[:, width:], pair[:, :width]], axis=1)
    return jnp.concatenate([pair, turned], axis=0)


def dot(a, b):
    return jnp.dot(a, b, preferred_element_type=jnp.float32)


def merge_kernel(
    order, own_in, *refs, points, width
):
    sides, (out, own, zc, out_v, in_sems, out_sems) = (refs[:5], refs[5:10]), refs[10:]
    piece = zc.shape[3]
    me = lax.axis_index("grp")
    box = lax.axis_index("box")
    x, z = lax.rem(me, 4), lax.div(me, 4)
    z_low, z_high = lax.rem(z, 2), lax.div(z, 2)
    parity = lax.rem(box, 2)
    twin = box + 1 - 2 * parity
    copies = [pltpu.make_async_copy(own_in, own, in_sems.at[0])]
    for side, arrays in enumerate(sides):
        for i, rows, zs, xs in PLACES:
            sem = in_sems.at[len(copies)]
            copies.append(pltpu.make_async_copy(arrays[i].at[rows], zc.at[side, zs, xs], sem))
    for c in copies:
        c.start()
    for c in copies:
        c.wait()

    def face_rows(side, holder, p):
        rows = []
        for j in range(MB):
            face = order[holder, j]
            src = p * 8 + lax.div(face, 2)
            zr = jnp.bitwise_xor(lax.div(src, 4), z)
            xr = jnp.bitwise_xor(lax.rem(src, 4), x)
            at = pl.multiple_of(lax.rem(face, 2) * BLK, BLK)
            rows.append(zc[side, zr, xr, pl.ds(at, BLK), :])
        return jnp.concatenate(rows, axis=0)

    zb = jnp.concatenate([face_rows(0, box, 0), face_rows(0, box, 1)], axis=1)
    zs = jnp.concatenate([face_rows(1, twin, 0), face_rows(1, twin, 1)], axis=1)
    first = lax.div(me * width, BLK)
    ext = jnp.float32(1.0)
    parts = []
    for j in range(MB):
        ext = jnp.where(order[box, j] == first, jnp.float32(0.0), ext)
    for p in range(2):
        rows = [
            own[p, pl.ds(pl.multiple_of(order[box, j] * BLK, BLK), BLK), :] for j in range(MB)
        ]
        parts.append(jnp.concatenate(rows, axis=0))
    start = jnp.concatenate(parts, axis=1).astype(jnp.float32) * ext

    def times(left, v, exact=False):
        high = v.astype(jnp.bfloat16)
        res = dot(left, stacked(high, width))
        if exact:
            return res
        low = (v - high.astype(jnp.float32)).astype(jnp.bfloat16)
        return res + dot(left, stacked(low, width))

    v = start
    for step in range(3):
        v = start + (1.0 / points) * times(zb, times(zs, v, exact=step == 0))
    resp = stacked(v.astype(jnp.bfloat16), width)
    echo = stacked(times(zs, v).astype(jnp.bfloat16), width)

    sent = []
    for xk in range(4):
        for zl in range(2):
            m = jnp.bitwise_xor(x, xk) + 4 * jnp.bitwise_xor(z_low, zl)
            rows = pl.ds(pl.multiple_of(m * piece, piece), piece)
            for side, right in ((0, echo), (1, resp)):
                zr = zc[side, zl + 2 * z_high, xk]
                zi = zc[side, zl + 2 - 2 * z_high, xk]
                acc = dot(jnp.concatenate([zr, zi], axis=1), right)
                half = jnp.bitwise_xor(parity, side)
                for p in range(2):
                    val = acc[:, p * width : (p + 1) * width]
                    if side == 0:
                        val = own[p, rows, :].astype(jnp.float32) * ext + val * (1.0 / points)
                    else:
                        val = val * -(points ** -0.5)
                    out_v[p, half, rows, :] = val.astype(jnp.bfloat16)
                view = (slice(None), half, rows)
                c = pltpu.make_async_copy(
                    out_v.at[view], out.at[view], out_sems.at[len(sent)]
                )
                c.start()
                sent.append(c)
    for c in sent:
        c.wait()


def shards(impedance, face_order):
    own_cols = impedance[:, 0, 0]
    points, width = own_cols.shape[1:]
    piece = 2 * points // 16
    box_here = lax.axis_index("box")
    own_order = lax.dynamic_index_in_dim(face_order, box_here, 0, keepdims=False)[0]
    spread = lax.all_to_all(own_cols.reshape(16, piece, width), "grp", 0, 0, tiled=True)
    mine = jnp.concatenate(
        [
            lax.dynamic_index_in_dim(spread, own_order[j] * BLK // width, 0, keepdims=False)
            for j in range(MB)
        ],
        axis=-1,
    )
    orders = face_order[:, 0]
    mine, orders = lax.optimization_barrier((mine, orders))
    z1, x1, x3, z3, x2, z2 = (
        exchange(mine, "grp", m)
        for m in (4, 1, 3, 12, 2, 8)
    )
    near = jnp.stack([x1, x2, x3])
    far = jnp.stack([z2, z3])
    every = jnp.stack([mine, z1, x1, x2, x3, z2, z3])
    late = [exchange(near, "grp", 4)]
    late += [exchange(far, "grp", k) for k in (1, 3, 2)]
    gathered = [every] + late
    gathered += [exchange(g, "box", 1) for g in gathered]
    anywhere = pl.BlockSpec(memory_space=pl.ANY)
    out = pl.pallas_call(
        functools.partial(merge_kernel, points=points, width=width),
        out_shape=jax.ShapeDtypeStruct((2, 2, points, width), jnp.bfloat16),
        in_specs=[pl.BlockSpec(memory_space=pltpu.SMEM)] + [anywhere] * 11,
        out_specs=anywhere,
        scratch_shapes=[
            pltpu.VMEM((2, points, width), jnp.bfloat16),
            pltpu.VMEM((2, 4, 4, piece, IFACE), jnp.bfloat16),
            pltpu.VMEM((2, 2, points, width), jnp.bfloat16),
            pltpu.SemaphoreType.DMA((17,)),
            pltpu.SemaphoreType.DMA((16,)),
        ],
        compiler_params=pltpu.CompilerParams(vmem_limit_bytes=24 << 20),
        name="merge",
    )(orders, own_cols, *gathered)
    return out.reshape(2, 1, 1, 2 * points, width)


def solution(mesh):
    in_specs = (P(None, "box", None, None, "grp"), P())
    out_specs = P(None, "box", None, None, "grp")
    return jax.shard_map(shards, mesh=mesh, in_specs=in_specs, out_specs=out_specs, check_vma=False)
```

```python
import functools

import jax
import jax.numpy as jnp
from jax import lax
from jax.experimental import pallas as pl
from jax.experimental.pallas import tpu as pltpu
from jax.sharding import PartitionSpec as P


BLK = 128
MB = 3
IFACE = MB * BLK

PLACES = (
    (0, pl.ds(0, 2), pl.ds(0, 2), 0),
    (0, pl.ds(2, 3), 0, pl.ds(1, 3)),
    (0, pl.ds(5, 2), pl.ds(2, 2), 0),
    (1, pl.ds(0, 3), 1, pl.ds(1, 3)),
    (2, 0, pl.ds(2, 2), 1),
    (2, 1, pl.ds(2, 2), 3),
    (2, 2, pl.ds(2, 2), 2),
)


def exchange(block, axis, mask):
    count = lax.axis_size(axis)
    return lax.ppermute(block, axis, [(i, i ^ mask) for i in range(count)])


def stacked(pair, width):
    turned = jnp.concatenate([-pair[:, width:], pair[:, :width]], axis=1)
    return jnp.concatenate([pair, turned], axis=0)


def dot(a, b):
    return jnp.dot(a, b, preferred_element_type=jnp.float32)


def merge_kernel(
    order, own_in, *refs, points, width
):
    sides, (out, own, zc, out_v, in_sems, out_sems) = (refs[:3], refs[3:6]), refs[6:]
    piece = zc.shape[3]
    me = lax.axis_index("grp")
    box = lax.axis_index("box")
    x, z = lax.rem(me, 4), lax.div(me, 4)
    z_low, z_high = lax.rem(z, 2), lax.div(z, 2)
    parity = lax.rem(box, 2)
    twin = box + 1 - 2 * parity
    copies = [pltpu.make_async_copy(own_in, own, in_sems.at[0])]
    for side, arrays in enumerate(sides):
        for i, rows, zs, xs in PLACES:
            sem = in_sems.at[len(copies)]
            copies.append(pltpu.make_async_copy(arrays[i].at[rows], zc.at[side, zs, xs], sem))
    for c in copies:
        c.start()
    for c in copies:
        c.wait()

    def face_rows(side, holder, p):
        rows = []
        for j in range(MB):
            face = order[holder, j]
            src = p * 8 + lax.div(face, 2)
            zr = jnp.bitwise_xor(lax.div(src, 4), z)
            xr = jnp.bitwise_xor(lax.rem(src, 4), x)
            at = pl.multiple_of(lax.rem(face, 2) * BLK, BLK)
            rows.append(zc[side, zr, xr, pl.ds(at, BLK), :])
        return jnp.concatenate(rows, axis=0)

    zb = jnp.concatenate([face_rows(0, box, 0), face_rows(0, box, 1)], axis=1)
    zs = jnp.concatenate([face_rows(1, twin, 0), face_rows(1, twin, 1)], axis=1)
    first = lax.div(me * width, BLK)
    ext = jnp.float32(1.0)
    parts = []
    for j in range(MB):
        ext = jnp.where(order[box, j] == first, jnp.float32(0.0), ext)
    for p in range(2):
        rows = [
            own[p, pl.ds(pl.multiple_of(order[box, j] * BLK, BLK), BLK), :] for j in range(MB)
        ]
        parts.append(jnp.concatenate(rows, axis=0))
    start = jnp.concatenate(parts, axis=1).astype(jnp.float32) * ext

    def times(left, v, exact=False):
        high = v.astype(jnp.bfloat16)
        res = dot(left, stacked(high, width))
        if exact:
            return res
        low = (v - high.astype(jnp.float32)).astype(jnp.bfloat16)
        return res + dot(left, stacked(low, width))

    v = start
    for step in range(3):
        v = start + (1.0 / points) * times(zb, times(zs, v, exact=step == 0))
    resp = stacked(v.astype(jnp.bfloat16), width)
    echo = stacked(times(zs, v).astype(jnp.bfloat16), width)

    sent = []
    for side, right in ((1, resp), (0, echo)):
        half = jnp.bitwise_xor(parity, side)
        for zl in range(2):
            zr = zc[side, zl + 2 * z_high].reshape(4 * piece, IFACE)
            zi = zc[side, zl + 2 - 2 * z_high].reshape(4 * piece, IFACE)
            acc = dot(jnp.concatenate([zr, zi], axis=1), right)
            for xk in range(4):
                m = jnp.bitwise_xor(x, xk) + 4 * jnp.bitwise_xor(z_low, zl)
                rows = pl.ds(pl.multiple_of(m * piece, piece), piece)
                for p in range(2):
                    val = acc[xk * piece : (xk + 1) * piece, p * width : (p + 1) * width]
                    if side == 0:
                        val = own[p, rows, :].astype(jnp.float32) * ext + val * (1.0 / points)
                    else:
                        val = val * -(points ** -0.5)
                    out_v[p, half, rows, :] = val.astype(jnp.bfloat16)
                view = (slice(None), half, rows)
                c = pltpu.make_async_copy(out_v.at[view], out.at[view], out_sems.at[len(sent)])
                c.start()
                sent.append(c)
    for c in sent:
        c.wait()


def shards(impedance, face_order):
    own_cols = impedance[:, 0, 0]
    points, width = own_cols.shape[1:]
    piece = 2 * points // 16
    box_here = lax.axis_index("box")
    own_order = lax.dynamic_index_in_dim(face_order, box_here, 0, keepdims=False)[0]
    spread = lax.all_to_all(own_cols.reshape(16, piece, width), "grp", 0, 0, tiled=True)
    mine = jnp.concatenate(
        [
            lax.dynamic_index_in_dim(spread, own_order[j] * BLK // width, 0, keepdims=False)
            for j in range(MB)
        ],
        axis=-1,
    )
    orders = face_order[:, 0]
    mine, orders = lax.optimization_barrier((mine, orders))
    z1, x1, x3, z3, x2, z2 = (
        exchange(mine, "grp", m)
        for m in (4, 1, 3, 12, 2, 8)
    )
    near = jnp.stack([x1, x2, x3])
    far = jnp.stack([z2, z3])
    every = jnp.stack([mine, z1, x1, x2, x3, z2, z3])
    beside = exchange(near, "grp", 4)
    both = jnp.stack([exchange(far, "grp", k) for k in (1, 3, 2)])
    gathered = [every, beside, both]
    gathered += [exchange(g, "box", 1) for g in gathered]
    anywhere = pl.BlockSpec(memory_space=pl.ANY)
    out = pl.pallas_call(
        functools.partial(merge_kernel, points=points, width=width),
        out_shape=jax.ShapeDtypeStruct((2, 2, points, width), jnp.bfloat16),
        in_specs=[pl.BlockSpec(memory_space=pltpu.SMEM)] + [anywhere] * 7,
        out_specs=anywhere,
        scratch_shapes=[
            pltpu.VMEM((2, points, width), jnp.bfloat16),
            pltpu.VMEM((2, 4, 4, piece, IFACE), jnp.bfloat16),
            pltpu.VMEM((2, 2, points, width), jnp.bfloat16),
            pltpu.SemaphoreType.DMA((15,)),
            pltpu.SemaphoreType.DMA((16,)),
        ],
        compiler_params=pltpu.CompilerParams(vmem_limit_bytes=24 << 20),
        name="merge",
    )(orders, own_cols, *gathered)
    return out.reshape(2, 1, 1, 2 * points, width)


def solution(mesh):
    in_specs = (P(None, "box", None, None, "grp"), P())
    out_specs = P(None, "box", None, None, "grp")
    return jax.shard_map(shards, mesh=mesh, in_specs=in_specs, out_specs=out_specs, check_vma=False)
```

```python
import functools

import jax
import jax.numpy as jnp
from jax import lax
from jax.experimental import pallas as pl
from jax.experimental.pallas import tpu as pltpu
from jax.sharding import PartitionSpec as P


BLK = 128
MB = 3
IFACE = MB * BLK

PLACES = (
    (0, pl.ds(0, 2), pl.ds(0, 2), 0),
    (0, pl.ds(2, 3), 0, pl.ds(1, 3)),
    (0, pl.ds(5, 2), pl.ds(2, 2), 0),
    (1, pl.ds(0, 3), 1, pl.ds(1, 3)),
    (1, pl.ds(3, 2), pl.ds(2, 2), 1),
    (1, pl.ds(5, 2), pl.ds(2, 2), 3),
    (1, pl.ds(7, 2), pl.ds(2, 2), 2),
)


def exchange(block, axis, mask):
    count = lax.axis_size(axis)
    return lax.ppermute(block, axis, [(i, i ^ mask) for i in range(count)])


def stacked(pair, width):
    turned = jnp.concatenate([-pair[:, width:], pair[:, :width]], axis=1)
    return jnp.concatenate([pair, turned], axis=0)


def dot(a, b):
    return jnp.dot(a, b, preferred_element_type=jnp.float32)


def merge_kernel(
    order, own_in, *refs, points, width
):
    sides, (out, own, zc, out_v, in_sems, out_sems) = (refs[:2], refs[2:4]), refs[4:]
    piece = zc.shape[3]
    me = lax.axis_index("grp")
    box = lax.axis_index("box")
    x, z = lax.rem(me, 4), lax.div(me, 4)
    z_low, z_high = lax.rem(z, 2), lax.div(z, 2)
    parity = lax.rem(box, 2)
    twin = box + 1 - 2 * parity
    copies = [pltpu.make_async_copy(own_in, own, in_sems.at[0])]
    for side, arrays in enumerate(sides):
        for i, rows, zs, xs in PLACES:
            sem = in_sems.at[len(copies)]
            copies.append(pltpu.make_async_copy(arrays[i].at[rows], zc.at[side, zs, xs], sem))
    for c in copies:
        c.start()
    for c in copies:
        c.wait()

    def face_rows(side, holder, p):
        rows = []
        for j in range(MB):
            face = order[holder, j]
            src = p * 8 + lax.div(face, 2)
            zr = jnp.bitwise_xor(lax.div(src, 4), z)
            xr = jnp.bitwise_xor(lax.rem(src, 4), x)
            at = pl.multiple_of(lax.rem(face, 2) * BLK, BLK)
            rows.append(zc[side, zr, xr, pl.ds(at, BLK), :])
        return jnp.concatenate(rows, axis=0)

    zb = jnp.concatenate([face_rows(0, box, 0), face_rows(0, box, 1)], axis=1)
    zs = jnp.concatenate([face_rows(1, twin, 0), face_rows(1, twin, 1)], axis=1)
    first = lax.div(me * width, BLK)
    ext = jnp.float32(1.0)
    parts = []
    for j in range(MB):
        ext = jnp.where(order[box, j] == first, jnp.float32(0.0), ext)
    for p in range(2):
        rows = [
            own[p, pl.ds(pl.multiple_of(order[box, j] * BLK, BLK), BLK), :] for j in range(MB)
        ]
        parts.append(jnp.concatenate(rows, axis=0))
    start = jnp.concatenate(parts, axis=1).astype(jnp.float32) * ext

    def times(left, v, exact=False):
        high = v.astype(jnp.bfloat16)
        res = dot(left, stacked(high, width))
        if exact:
            return res
        low = (v - high.astype(jnp.float32)).astype(jnp.bfloat16)
        return res + dot(left, stacked(low, width))

    v = start
    for step in range(3):
        v = start + (1.0 / points) * times(zb, times(zs, v, exact=step == 0))
    resp = stacked(v.astype(jnp.bfloat16), width)
    echo = stacked(times(zs, v).astype(jnp.bfloat16), width)

    sent = []
    for side, right in ((1, resp), (0, echo)):
        half = jnp.bitwise_xor(parity, side)
        for zl in range(2):
            zr = zc[side, zl + 2 * z_high].reshape(4 * piece, IFACE)
            zi = zc[side, zl + 2 - 2 * z_high].reshape(4 * piece, IFACE)
            acc = dot(jnp.concatenate([zr, zi], axis=1), right)
            for xk in range(4):
                m = jnp.bitwise_xor(x, xk) + 4 * jnp.bitwise_xor(z_low, zl)
                rows = pl.ds(pl.multiple_of(m * piece, piece), piece)
                for p in range(2):
                    val = acc[xk * piece : (xk + 1) * piece, p * width : (p + 1) * width]
                    if side == 0:
                        val = own[p, rows, :].astype(jnp.float32) * ext + val * (1.0 / points)
                    else:
                        val = val * -(points ** -0.5)
                    out_v[p, half, rows, :] = val.astype(jnp.bfloat16)
                view = (slice(None), half, rows)
                c = pltpu.make_async_copy(out_v.at[view], out.at[view], out_sems.at[len(sent)])
                c.start()
                sent.append(c)
    for c in sent:
        c.wait()


def shards(impedance, face_order):
    own_cols = impedance[:, 0, 0]
    points, width = own_cols.shape[1:]
    piece = 2 * points // 16
    box_here = lax.axis_index("box")
    own_order = lax.dynamic_index_in_dim(face_order, box_here, 0, keepdims=False)[0]
    spread = lax.all_to_all(own_cols.reshape(16, piece, width), "grp", 0, 0, tiled=True)
    mine = jnp.concatenate(
        [
            lax.dynamic_index_in_dim(spread, own_order[j] * BLK // width, 0, keepdims=False)
            for j in range(MB)
        ],
        axis=-1,
    )
    orders = face_order[:, 0]
    mine, orders = lax.optimization_barrier((mine, orders))
    z1, x1, x3, z3, x2, z2 = (
        exchange(mine, "grp", m)
        for m in (4, 1, 3, 12, 2, 8)
    )
    near = jnp.stack([x1, x2, x3])
    far = jnp.stack([z2, z3])
    every = jnp.stack([mine, z1, x1, x2, x3, z2, z3])
    late = [exchange(near, "grp", 4)]
    late += [exchange(far, "grp", k) for k in (1, 3, 2)]
    gathered = [every, jnp.concatenate(late, axis=0)]
    gathered += [exchange(g, "box", 1) for g in gathered]
    anywhere = pl.BlockSpec(memory_space=pl.ANY)
    out = pl.pallas_call(
        functools.partial(merge_kernel, points=points, width=width),
        out_shape=jax.ShapeDtypeStruct((2, 2, points, width), jnp.bfloat16),
        in_specs=[pl.BlockSpec(memory_space=pltpu.SMEM)] + [anywhere] * 5,
        out_specs=anywhere,
        scratch_shapes=[
            pltpu.VMEM((2, points, width), jnp.bfloat16),
            pltpu.VMEM((2, 4, 4, piece, IFACE), jnp.bfloat16),
            pltpu.VMEM((2, 2, points, width), jnp.bfloat16),
            pltpu.SemaphoreType.DMA((15,)),
            pltpu.SemaphoreType.DMA((16,)),
        ],
        compiler_params=pltpu.CompilerParams(vmem_limit_bytes=24 << 20),
        name="merge",
    )(orders, own_cols, *gathered)
    return out.reshape(2, 1, 1, 2 * points, width)


def solution(mesh):
    in_specs = (P(None, "box", None, None, "grp"), P())
    out_specs = P(None, "box", None, None, "grp")
    return jax.shard_map(shards, mesh=mesh, in_specs=in_specs, out_specs=out_specs, check_vma=False)
```

```python
import functools

import jax
import jax.numpy as jnp
from jax import lax
from jax.experimental import pallas as pl
from jax.experimental.pallas import tpu as pltpu
from jax.sharding import PartitionSpec as P


BLK = 128
MB = 3
IFACE = MB * BLK

LATE = {(1, 1): 0, (1, 2): 1, (1, 3): 2, (2, 1): 3, (3, 1): 4, (2, 3): 5, (3, 3): 6, (2, 2): 7, (3, 2): 8}


def exchange(block, axis, mask):
    count = lax.axis_size(axis)
    return lax.ppermute(block, axis, [(i, i ^ mask) for i in range(count)])


def stacked(pair, width):
    turned = jnp.concatenate([-pair[:, width:], pair[:, :width]], axis=1)
    return jnp.concatenate([pair, turned], axis=0)


def dot(a, b):
    return jnp.dot(a, b, preferred_element_type=jnp.float32)


def merge_kernel(
    order, own, *refs, points, width
):
    sides, (out, zf, out_v, in_sems, out_sems) = (refs[:2], refs[2:4]), refs[4:]
    piece = refs[0].shape[1]
    me = lax.axis_index("grp")
    box = lax.axis_index("box")
    x, z = lax.rem(me, 4), lax.div(me, 4)
    z_low, z_high = lax.rem(z, 2), lax.div(z, 2)
    parity = lax.rem(box, 2)
    twin = box + 1 - 2 * parity
    waits = []
    for side, (every, late) in enumerate(sides):
        holder = twin if side else box
        for j in range(MB):
            face = order[holder, j]
            at = pl.multiple_of(lax.rem(face, 2) * BLK, BLK)
            for p in range(2):
                src = p * 8 + lax.div(face, 2)
                zr = jnp.bitwise_xor(lax.div(src, 4), z)
                xr = jnp.bitwise_xor(lax.rem(src, 4), x)
                dst = zf.at[side, pl.ds(j * BLK, BLK), pl.ds(p * IFACE, IFACE)]
                sem = in_sems.at[len(waits)]
                near = jnp.where(zr == 0, jnp.where(xr == 0, 0, 1 + xr), jnp.where(zr == 1, 1, 3 + zr))
                pair = jnp.where(xr == 1, 3, jnp.where(xr == 3, 5, 7)) + zr - 2
                far = jnp.where(zr == 1, xr - 1, pair)
                is_near = (zr == 0) | (xr == 0)

                @pl.when(is_near)
                def _(near=near, at=at, dst=dst, sem=sem, every=every):
                    pltpu.make_async_copy(every.at[near, pl.ds(at, BLK)], dst, sem).start()

                @pl.when(jnp.logical_not(is_near))
                def _(far=far, at=at, dst=dst, sem=sem, late=late):
                    pltpu.make_async_copy(late.at[far, pl.ds(at, BLK)], dst, sem).start()

                waits.append(pltpu.make_async_copy(every.at[0, pl.ds(0, BLK)], dst, sem))
    for c in waits:
        c.wait()
    zb, zs = zf[0], zf[1]
    first = lax.div(me * width, BLK)
    ext = jnp.float32(1.0)
    parts = []
    for j in range(MB):
        ext = jnp.where(order[box, j] == first, jnp.float32(0.0), ext)
    for p in range(2):
        rows = [
            own[p, pl.ds(pl.multiple_of(order[box, j] * BLK, BLK), BLK), :] for j in range(MB)
        ]
        parts.append(jnp.concatenate(rows, axis=0))
    start = jnp.concatenate(parts, axis=1).astype(jnp.float32) * ext

    def times(left, v, exact=False):
        high = v.astype(jnp.bfloat16)
        res = dot(left, stacked(high, width))
        if exact:
            return res
        low = (v - high.astype(jnp.float32)).astype(jnp.bfloat16)
        return res + dot(left, stacked(low, width))

    v = start
    for step in range(3):
        v = start + (1.0 / points) * times(zb, times(zs, v, exact=step == 0))
    resp = stacked(v.astype(jnp.bfloat16), width)
    echo = stacked(times(zs, v).astype(jnp.bfloat16), width)

    sent = []
    for side, right in ((1, resp), (0, echo)):
        half = jnp.bitwise_xor(parity, side)
        every, late = sides[side]
        where_is = {(zd, xd): (late, LATE[zd, xd]) for zd in range(1, 4) for xd in range(1, 4)}
        where_is.update({(0, xd): (every, 1 + xd if xd else 0) for xd in range(4)})
        where_is.update({(1, 0): (every, 1), (2, 0): (every, 5), (3, 0): (every, 6)})
        turn = jnp.concatenate([right[IFACE:], right[:IFACE]], axis=0)
        right = jnp.where(z_high == 0, right, turn)
        for zl in range(2):
            columns = []
            for zd in (zl, zl + 2):
                rows = [where_is[zd, xd] for xd in range(4)]
                columns.append(jnp.concatenate([arr[i] for arr, i in rows], axis=0))
            acc = dot(jnp.concatenate(columns, axis=1), right)
            for xk in range(4):
                m = jnp.bitwise_xor(x, xk) + 4 * jnp.bitwise_xor(z_low, zl)
                rows = pl.ds(pl.multiple_of(m * piece, piece), piece)
                for p in range(2):
                    val = acc[xk * piece : (xk + 1) * piece, p * width : (p + 1) * width]
                    if side == 0:
                        val = own[p, rows, :].astype(jnp.float32) * ext + val * (1.0 / points)
                    else:
                        val = val * -(points ** -0.5)
                    out_v[p, half, rows, :] = val.astype(jnp.bfloat16)
                view = (slice(None), half, rows)
                c = pltpu.make_async_copy(out_v.at[view], out.at[view], out_sems.at[len(sent)])
                c.start()
                sent.append(c)
    for c in sent:
        c.wait()


def shards(impedance, face_order):
    own_cols = impedance[:, 0, 0]
    points, width = own_cols.shape[1:]
    piece = 2 * points // 16
    box_here = lax.axis_index("box")
    own_order = lax.dynamic_index_in_dim(face_order, box_here, 0, keepdims=False)[0]
    spread = lax.all_to_all(own_cols.reshape(16, piece, width), "grp", 0, 0, tiled=True)
    mine = jnp.concatenate(
        [
            lax.dynamic_index_in_dim(spread, own_order[j] * BLK // width, 0, keepdims=False)
            for j in range(MB)
        ],
        axis=-1,
    )
    orders = face_order[:, 0]
    mine, orders = lax.optimization_barrier((mine, orders))
    z1, x1, x3, z3, x2, z2 = (
        exchange(mine, "grp", m)
        for m in (4, 1, 3, 12, 2, 8)
    )
    near = jnp.stack([x1, x2, x3])
    far = jnp.stack([z2, z3])
    every = jnp.stack([mine, z1, x1, x2, x3, z2, z3])
    late = [exchange(near, "grp", 4)]
    late += [exchange(far, "grp", k) for k in (1, 3, 2)]
    gathered = [every, jnp.concatenate(late, axis=0)]
    gathered += [exchange(g, "box", 1) for g in gathered]
    anywhere = pl.BlockSpec(memory_space=pl.ANY)
    vmem = pl.BlockSpec(memory_space=pltpu.VMEM)
    out = pl.pallas_call(
        functools.partial(merge_kernel, points=points, width=width),
        out_shape=jax.ShapeDtypeStruct((2, 2, points, width), jnp.bfloat16),
        in_specs=[pl.BlockSpec(memory_space=pltpu.SMEM)] + [vmem] * 5,
        out_specs=anywhere,
        scratch_shapes=[
            pltpu.VMEM((2, IFACE, 2 * IFACE), jnp.bfloat16),
            pltpu.VMEM((2, 2, points, width), jnp.bfloat16),
            pltpu.SemaphoreType.DMA((12,)),
            pltpu.SemaphoreType.DMA((16,)),
        ],
        compiler_params=pltpu.CompilerParams(vmem_limit_bytes=24 << 20),
        name="merge",
    )(orders, own_cols, *gathered)
    return out.reshape(2, 1, 1, 2 * points, width)


def solution(mesh):
    in_specs = (P(None, "box", None, None, "grp"), P())
    out_specs = P(None, "box", None, None, "grp")
    return jax.shard_map(shards, mesh=mesh, in_specs=in_specs, out_specs=out_specs, check_vma=False)
```
